32 devices in a mesh: prow: 8 (over z, x), pcol: 4 (over y, core).
Axes of the slice: x: 2, y: 2, z: 4, core: 2. Of those that a mesh axis runs over, the one named last changes fastest.
Arguments:
- system: bfloat16 [6144, 65536], P('prow', 'pcol'), may hold values from -6 to 6
- row_outer: float32 [6144], P('prow'), may hold values from 0.5 to 2
- row_inner: float32 [6144], P('prow'), may hold values from 0.5 to 2
- col_outer: float32 [65536], P('pcol'), may hold values from 0.5 to 2
- col_inner: float32 [65536], P('pcol'), may hold values from 0.5 to 2
- diag_inverse: bfloat16 [512, 512], replicated, may hold values from -0.01171875 to 0.01171875
Outputs:
- trailing: bfloat16 [6144, 65536], P('prow', 'pcol')
The draws below stay inside these ranges and needn't reach their ends.
All inputs are finite; a program needn't handle non-finite values.
Results may differ from the reference program's by a relative error of at most 0.0089.
Values may be sent and summed in bfloat16 or wider, within the bound.
A program may use at most 192 MiB of HBM per device.

```python
import math
import jax
import jax.numpy as jnp

N = 65536
PANEL = 512
M = 6144


def level_of(own_key, shape, pieces, low, largest):
    factor_of = 1.0
    for dim, parts in pieces:
        draws = jax.random.uniform(jax.random.fold_in(jax.random.fold_in(own_key, 6), dim), (parts,), jnp.float32, low / len(pieces), largest / len(pieces))
        factor_of = factor_of * jnp.repeat(jnp.exp(draws), shape[dim] // parts).reshape((-1,) + (1,) * (len(shape) - 1 - dim))
    return factor_of


def normal_values(key, extent, spread, bound, split=(), held_as=jnp.bfloat16):
    result = spread * jax.random.normal(key, extent, jnp.float32)
    if split:
        result = result * level_of(key, extent, split, -0.22, 0.18)
    return jnp.clip(result, -bound, bound).astype(held_as)


def setup_inputs(seed: int = 0) -> dict:
    splits = jax.random.split(jax.random.key(seed), 7)
    system = normal_values(splits[0], (M, N), 1.0, 6.0, ((0, 8), (1, 4)))
    row_outer = jnp.clip(jnp.exp(math.log(2.0) - 1.3862944 * jax.random.uniform(splits[1], (M,), jnp.float32) ** level_of(splits[1], (M,), ((0, 8),), -0.2, 0.2)), 0.5, 2.0)
    row_inner = jnp.clip(jnp.exp(math.log(2.0) - 1.3862944 * jax.random.uniform(splits[2], (M,), jnp.float32) ** level_of(splits[2], (M,), ((0, 8),), -0.2, 0.2)), 0.5, 2.0)
    col_outer = jnp.clip(jnp.exp(math.log(2.0) - 1.3862944 * jax.random.uniform(splits[3], (N,), jnp.float32) ** level_of(splits[3], (N,), ((0, 4),), -0.2, 0.2)), 0.5, 2.0)
    col_inner = jnp.clip(jnp.exp(math.log(2.0) - 1.3862944 * jax.random.uniform(splits[4], (N,), jnp.float32) ** level_of(splits[4], (N,), ((0, 4),), -0.2, 0.2)), 0.5, 2.0)
    diag_inverse = normal_values(splits[5], (PANEL, PANEL), (PANEL * PANEL) ** -0.5, 0.01171875)
    return dict(system=system, row_outer=row_outer, row_inner=row_inner, col_outer=col_outer, col_inner=col_inner, diag_inverse=diag_inverse)


root_half = 0.7071067811865476


def mix_rows(values, weights, half):
    rows, cols = values.shape
    blocks = values.astype(jnp.float32).reshape(rows // (2 * half), 2, half, cols)
    scales = weights.reshape(rows // (2 * half), 2, half, 1)
    upper = scales[:, 0] * (blocks[:, 0] + blocks[:, 1]) * root_half
    lower = scales[:, 1] * (blocks[:, 0] - blocks[:, 1]) * root_half
    return jnp.stack([upper, lower], axis=1).reshape(rows, cols).astype(jnp.bfloat16)


def mix_cols(values, weights, half):
    rows, cols = values.shape
    blocks = values.astype(jnp.float32).reshape(rows, cols // (2 * half), 2, half)
    scales = weights.reshape(1, cols // (2 * half), 2, half)
    upper = scales[:, :, 0] * (blocks[:, :, 0] + blocks[:, :, 1]) * root_half
    lower = scales[:, :, 1] * (blocks[:, :, 0] - blocks[:, :, 1]) * root_half
    return jnp.stack([upper, lower], axis=2).reshape(rows, cols).astype(jnp.bfloat16)


def reference(system, row_outer, row_inner, col_outer, col_inner, diag_inverse):
    first = mix_rows(system, row_outer, M // 2)
    second = mix_rows(first, row_inner, M // 4)
    third = mix_cols(second, col_outer, N // 2)
    transformed = mix_cols(third, col_inner, N // 4)
    left = jnp.dot(transformed[:, :PANEL], diag_inverse, preferred_element_type=jnp.float32).astype(jnp.bfloat16)
    update = jnp.dot(left, transformed[:PANEL, :], preferred_element_type=jnp.float32)
    return (transformed.astype(jnp.float32) - update).astype(jnp.bfloat16)
```

```python
import functools

import jax
import jax.numpy as jnp
from jax import lax
from jax.experimental import pallas as pl
from jax.experimental.pallas import tpu as pltpu
from jax.sharding import PartitionSpec as P

root_half = 0.7071067811865476
MESH = pl.DeviceIdType.MESH
WIDTH = 512
STRIP = 32
SLOTS = 4
LAST = 5


def kernel(
    K, width, panel, R, Q,
    system, row_coef, col_coef,
    full, lead, leading,
    s_buf, ra, tb, rb, m_buf, rc, rd1, rd2, e_buf, k_buf, l_buf,
    load_sem, a_send, a_recv, b_send, b_recv, m_send, c_recv, d1_recv, d2_send, d2_recv,
    e_send, e_recv, l_send, l_recv, k_sem, lk_sem, f_send, f_recv, g_send, g_recv,
    cred_a, cred_b, cred_c, cred_d,
):
    rows = system.shape[0]
    C = Q // 4
    prow = lax.axis_index("prow")
    pcol = lax.axis_index("pcol")
    quarter = prow // R
    rank = prow % R
    col_quarter = pcol // C
    inner = (quarter == 1) | (quarter == 2)
    outer = (quarter == 0) | (quarter == 3)
    first_rank = rank == 0

    y_dev = (prow, lax.rem(pcol + 2 * C, Q))
    core_dev = (prow, jnp.where(col_quarter % 2 == 0, pcol + C, pcol - C))
    edge_dev = (jnp.where(quarter % 2 == 0, prow + R, prow - R), pcol)
    mid_dev = ((3 - quarter) * R + rank, pcol)

    def signal(sem, device):
        pl.semaphore_signal(sem, inc=1, device_id=device, device_id_type=MESH)

    barrier = pltpu.get_barrier_semaphore()
    for d in range(1, Q):
        signal(barrier, (prow, lax.rem(pcol + d, Q)))
    for d in range(1, R):
        signal(barrier, (quarter * R + lax.rem(rank + d, R), pcol))
    signal(barrier, edge_dev)
    signal(barrier, mid_dev)
    pl.semaphore_wait(barrier, Q - 1 + R - 1 + 2)

    def at(c):
        return pl.ds(pl.multiple_of(c * width, width), width)

    def remote(src, dst, send, recv, device):
        return pltpu.make_async_remote_copy(
            src_ref=src, dst_ref=dst, send_sem=send, recv_sem=recv, device_id=device, device_id_type=MESH
        )

    def load(c):
        return pltpu.make_async_copy(system.at[:, at(c)], s_buf.at[c % SLOTS], load_sem.at[c % SLOTS])

    def a_copy(c):
        k = c % SLOTS
        return remote(s_buf.at[k], ra.at[k], a_send.at[k], a_recv.at[k], y_dev)

    def b_copy(c):
        k = c % 2
        return remote(tb.at[k], rb.at[k], b_send.at[k], b_recv.at[k], core_dev)

    def c_copy(c):
        k = c % SLOTS
        return remote(m_buf.at[k], rc.at[k], m_send.at[k], c_recv.at[k], edge_dev)

    def d1_copy(c):
        k = c % SLOTS
        return remote(m_buf.at[k], rd1.at[k], m_send.at[k], d1_recv.at[k], mid_dev)

    def d2_copy(c):
        k = c % SLOTS
        return remote(rc.at[k], rd2.at[k], d2_send.at[k], d2_recv.at[k], mid_dev)

    def e_copy(c):
        k = c % 2
        return remote(e_buf.at[k], full.at[:, at(c)], e_send.at[k], e_recv.at[c], edge_dev)

    def l_copy(c):
        k = c % 2
        return remote(l_buf.at[k], lead.at[:, at(c)], l_send.at[k], l_recv.at[c], edge_dev)

    def k_copy(c):
        return pltpu.make_async_copy(k_buf.at[c % 2], full.at[:, at(c)], k_sem.at[c % 2])

    def lk_copy(c):
        return pltpu.make_async_copy(l_buf.at[c % 2], lead.at[:, at(c)], lk_sem.at[c % 2])

    def f_copy(c, d, from_hbm):
        src = lead.at[:, at(c)] if from_hbm else l_buf.at[c % 2]
        return remote(src, lead.at[:, at(c)], f_send.at[c % 2, d - 1], f_recv.at[c], (quarter * R + d, pcol))

    def g_copy(d):
        return remote(full.at[:, pl.ds(0, panel)], leading, g_send.at[d - 1], g_recv.at[0], (prow, d))

    def mix(mine, got, out, c, which):
        u = col_coef[which : which + 1, at(c)]
        v = col_coef[which + 1 : which + 2, at(c)]

        @pl.loop(0, rows // STRIP)
        def _(j):
            r = pl.ds(pl.multiple_of(j * STRIP, STRIP), STRIP)
            x = mine[r, :].astype(jnp.float32)
            y = got[r, :].astype(jnp.float32)
            out[r, :] = (u * x + v * y).astype(jnp.bfloat16)

    def combine(k, outs, strips):
        @pl.loop(0, strips)
        def _(j):
            r = pl.ds(pl.multiple_of(j * STRIP, STRIP), STRIP)
            w = row_coef[r, :]
            o = m_buf[k, r, :].astype(jnp.float32)
            n = rc[k, r, :].astype(jnp.float32)
            a = rd1[k, r, :].astype(jnp.float32)
            f = rd2[k, r, :].astype(jnp.float32)
            for out, b in outs:
                total = w[:, b : b + 1] * o + w[:, b + 1 : b + 2] * n
                total += w[:, b + 2 : b + 3] * a + w[:, b + 3 : b + 4] * f
                out[r, :] = total.astype(jnp.bfloat16)

    for c in range(3):
        load(c).start()
    for c in range(2):
        load(c).wait()
        a_copy(c).start()

    def body(i, carry):
        @pl.when(i + 3 < K)
        def _():
            load(i + 3).start()

        @pl.when(i + 2 < K)
        def _():
            c = i + 2
            load(c).wait()

            @pl.when(c >= SLOTS)
            def _():
                pl.semaphore_wait(cred_a, 1)

            a_copy(c).start()

        @pl.when(i < K)
        def _():
            c = i
            a_copy(c).wait_recv()

            @pl.when(c >= 2)
            def _():
                b_copy(c - 2).wait_send()

            mix(s_buf.at[c % SLOTS], ra.at[c % SLOTS], tb.at[c % 2], c, 0)
            a_copy(c).wait_send()

            @pl.when(c + SLOTS < K)
            def _():
                signal(cred_a, y_dev)

            @pl.when(c >= 2)
            def _():
                pl.semaphore_wait(cred_b, 1)

            b_copy(c).start()
            b_copy(c).wait_recv()

            @pl.when(outer & (c >= SLOTS))
            def _():
                c_copy(c - SLOTS).wait_send()

            mix(tb.at[c % 2], rb.at[c % 2], m_buf.at[c % SLOTS], c, 2)

            @pl.when(c + 2 < K)
            def _():
                signal(cred_b, core_dev)

            @pl.when(outer)
            def _():
                @pl.when(c >= SLOTS)
                def _():
                    pl.semaphore_wait(cred_c, 1)

                c_copy(c).start()

            @pl.when(inner)
            def _():
                @pl.when(c >= SLOTS)
                def _():
                    pl.semaphore_wait(cred_d, 1)

                d1_copy(c).start()

        @pl.when(inner & (i >= 1) & (i - 1 < K))
        def _():
            c = i - 1
            c_copy(c).wait_recv()
            d2_copy(c).start()

        @pl.when(inner & (i >= 3) & (i - 3 < K))
        def _():
            c = i - 3
            d1_copy(c).wait()
            d2_copy(c).wait()

            @pl.when(c >= 2)
            def _():
                e_copy(c - 2).wait_send()
                k_copy(c - 2).wait()

            combine(c % SLOTS, ((e_buf.at[c % 2], 0), (k_buf.at[c % 2], 4)), rows // STRIP)
            e_copy(c).start()
            k_copy(c).start()

            @pl.when(first_rank)
            def _():
                @pl.when(c >= 2)
                def _():
                    l_copy(c - 2).wait_send()
                    lk_copy(c - 2).wait()
                    for d in range(1, R):
                        f_copy(c - 2, d, False).wait_send()

                combine(c % SLOTS, ((l_buf.at[c % 2], 8),), panel // STRIP)
                l_copy(c).start()
                lk_copy(c).start()
                for d in range(1, R):
                    f_copy(c, d, False).start()

            @pl.when(c + SLOTS < K)
            def _():
                signal(cred_c, edge_dev)
                signal(cred_d, mid_dev)

        @pl.when(outer & (i >= LAST) & (i - LAST < K))
        def _():
            c = i - LAST
            e_copy(c).wait_recv()

            @pl.when(first_rank)
            def _():
                l_copy(c).wait_recv()

                @pl.when(c >= 2)
                def _():
                    for d in range(1, R):
                        f_copy(c - 2, d, True).wait_send()

                for d in range(1, R):
                    f_copy(c, d, True).start()

        @pl.when((pcol == 0) & (i == panel // width + 4))
        def _():
            for d in range(1, Q):
                g_copy(d).start()

        return carry

    lax.fori_loop(0, K + LAST, body, 0)

    for c in (K - 2, K - 1):
        b_copy(c).wait_send()

        @pl.when(inner)
        def _():
            e_copy(c).wait_send()
            k_copy(c).wait()

            @pl.when(first_rank)
            def _():
                l_copy(c).wait_send()
                lk_copy(c).wait()
                for d in range(1, R):
                    f_copy(c, d, False).wait_send()

        @pl.when(outer & first_rank)
        def _():
            for d in range(1, R):
                f_copy(c, d, True).wait_send()

    @pl.when(outer)
    def _():
        for c in range(K - SLOTS, K):
            c_copy(c).wait_send()

    @pl.when(rank > 0)
    def _():
        @pl.loop(0, K)
        def _(c):
            f_copy(c, 0, True).wait_recv() if R == 1 else f_copy(c, 1, True).wait_recv()

    @pl.when(pcol == 0)
    def _():
        for d in range(1, Q):
            g_copy(d).wait_send()

    @pl.when(pcol > 0)
    def _():
        g_copy(1).wait_recv()


def per_device(system, row_outer, row_inner, col_outer, col_inner, diag_inverse):
    panel = diag_inverse.shape[0]
    rows, cols = system.shape
    R = lax.axis_size("prow") // 4
    Q = lax.axis_size("pcol")
    C = Q // 4
    width = min(WIDTH, panel, cols // 8)
    K = cols // width
    f32, bf16 = jnp.float32, jnp.bfloat16
    assert lax.axis_size("prow") % 4 == 0 and Q % 4 == 0
    assert cols % width == 0 and panel % width == 0 and K >= panel // width + 4
    assert panel <= rows and panel % STRIP == 0 and rows % STRIP == 0
    quarter = lax.axis_index("prow") // R
    col_quarter = lax.axis_index("pcol") // C

    def hops(pairs):
        return [(a * R + r, b * R + r) for a, b in pairs for r in range(R)]

    is1 = quarter == 1
    own = jnp.stack([row_outer, row_inner])
    near = lax.ppermute(own, "prow", hops([(0, 1), (3, 2)]))
    other = lax.ppermute(jnp.concatenate([own, near]), "prow", hops([(1, 2), (2, 1)]))
    across, far = other[:2], other[2:]
    w0 = jnp.where(is1, near, far)
    w1 = jnp.where(is1, own, across)
    w2 = jnp.where(is1, across, own)
    w3 = jnp.where(is1, far, near)
    outer_a, inner_u = jnp.where(is1, w0, w2)
    outer_b, inner_d = jnp.where(is1, w1, w3)
    u0, u1 = 0.5 * inner_u * outer_a, 0.5 * inner_u * outer_b
    d0, d1 = 0.5 * inner_d * outer_a, 0.5 * inner_d * outer_b
    l0, l1 = 0.5 * w0[1] * w0[0], 0.5 * w0[1] * w1[0]
    one = jnp.stack([u1, u0, u0, u1, -d1, d0, d0, -d1, l1, l0, l0, l1])
    two = jnp.stack([-d0, d1, -d1, d0, -u0, -u1, u1, u0, l0, l1, l1, l0])
    row_coef = jnp.where(is1, one, two).T

    outer_c, inner_c = col_outer * root_half, col_inner * root_half
    col_coef = jnp.stack(
        [
            jnp.where(col_quarter < 2, outer_c, -outer_c),
            outer_c,
            jnp.where(col_quarter % 2 == 0, inner_c, -inner_c),
            inner_c,
        ]
    )

    dma = lambda *shape: pltpu.SemaphoreType.DMA(shape)
    block = lambda n, height: pltpu.VMEM((n, height, width), bf16)
    any_spec = pl.BlockSpec(memory_space=pl.ANY)
    vmem_spec = pl.BlockSpec(memory_space=pltpu.VMEM)
    full, lead, leading = pl.pallas_call(
        functools.partial(kernel, K, width, panel, R, Q),
        out_shape=(
            jax.ShapeDtypeStruct((rows, cols), bf16),
            jax.ShapeDtypeStruct((panel, cols), bf16),
            jax.ShapeDtypeStruct((rows, panel), bf16),
        ),
        in_specs=[any_spec, vmem_spec, vmem_spec],
        out_specs=(any_spec, any_spec, any_spec),
        scratch_shapes=[
            block(SLOTS, rows), block(SLOTS, rows), block(2, rows), block(2, rows),
            block(SLOTS, rows), block(SLOTS, rows), block(SLOTS, rows), block(SLOTS, rows),
            block(2, rows), block(2, rows), block(2, panel),
            dma(SLOTS), dma(SLOTS), dma(SLOTS), dma(2), dma(2), dma(SLOTS), dma(SLOTS), dma(SLOTS),
            dma(SLOTS), dma(SLOTS),
            dma(2), dma(K), dma(2), dma(K), dma(2), dma(2), dma(2, max(R - 1, 1)), dma(K), dma(Q - 1), dma(1),
            pltpu.SemaphoreType.REGULAR, pltpu.SemaphoreType.REGULAR,
            pltpu.SemaphoreType.REGULAR, pltpu.SemaphoreType.REGULAR,
        ],
        compiler_params=pltpu.CompilerParams(
            collective_id=0, has_side_effects=True, vmem_limit_bytes=60 * 1024 * 1024
        ),
    )(system, row_coef, col_coef)
    leading = jnp.where(lax.axis_index("pcol") == 0, full[:, :panel], leading)
    left = jnp.dot(leading, diag_inverse, preferred_element_type=f32).astype(bf16)
    update = jnp.dot(left, lead, preferred_element_type=f32)
    return (full.astype(f32) - update).astype(bf16)


def solution(mesh):
    in_specs = (P("prow", "pcol"), P("prow"), P("prow"), P("pcol"), P("pcol"), P())
    out_specs = P("prow", "pcol")
    return jax.shard_map(
        per_device, mesh=mesh, in_specs=in_specs, out_specs=out_specs, check_vma=False
    )
```

```python
import functools

import jax
import jax.numpy as jnp
from jax import lax
from jax.experimental import pallas as pl
from jax.experimental.pallas import tpu as pltpu
from jax.sharding import PartitionSpec as P

root_half = 0.7071067811865476
MESH = pl.DeviceIdType.MESH
WIDTH = 128
STRIP = 32
SLOTS = 4
LAST = 5


def kernel(
    K, width, panel, R, Q,
    system, row_coef, col_coef,
    full, lead, leading,
    s_buf, ra, tb, rb, m_buf, rc, rd1, rd2, e_buf, k_buf, l_buf,
    load_sem, a_send, a_recv, b_send, b_recv, m_send, c_recv, d1_recv, d2_send, d2_recv,
    e_send, e_recv, l_send, l_recv, k_sem, lk_sem, f_send, f_recv, g_send, g_recv,
    cred_a, cred_b, cred_c, cred_d,
):
    rows = system.shape[0]
    C = Q // 4
    prow = lax.axis_index("prow")
    pcol = lax.axis_index("pcol")
    quarter = prow // R
    rank = prow % R
    col_quarter = pcol // C
    inner = (quarter == 1) | (quarter == 2)
    outer = (quarter == 0) | (quarter == 3)
    first_rank = rank == 0

    y_dev = (prow, lax.rem(pcol + 2 * C, Q))
    core_dev = (prow, jnp.where(col_quarter % 2 == 0, pcol + C, pcol - C))
    edge_dev = (jnp.where(quarter % 2 == 0, prow + R, prow - R), pcol)
    mid_dev = ((3 - quarter) * R + rank, pcol)

    def signal(sem, device):
        pl.semaphore_signal(sem, inc=1, device_id=device, device_id_type=MESH)

    barrier = pltpu.get_barrier_semaphore()
    for d in range(1, Q):
        signal(barrier, (prow, lax.rem(pcol + d, Q)))
    for d in range(1, R):
        signal(barrier, (quarter * R + lax.rem(rank + d, R), pcol))
    signal(barrier, edge_dev)
    signal(barrier, mid_dev)
    pl.semaphore_wait(barrier, Q - 1 + R - 1 + 2)

    def at(c):
        return pl.ds(pl.multiple_of(c * width, width), width)

    def remote(src, dst, send, recv, device):
        return pltpu.make_async_remote_copy(
            src_ref=src, dst_ref=dst, send_sem=send, recv_sem=recv, device_id=device, device_id_type=MESH
        )

    def load(c):
        return pltpu.make_async_copy(system.at[:, at(c)], s_buf.at[c % SLOTS], load_sem.at[c % SLOTS])

    def a_copy(c):
        k = c % SLOTS
        return remote(s_buf.at[k], ra.at[k], a_send.at[k], a_recv.at[k], y_dev)

    def b_copy(c):
        k = c % 2
        return remote(tb.at[k], rb.at[k], b_send.at[k], b_recv.at[k], core_dev)

    def c_copy(c):
        k = c % SLOTS
        return remote(m_buf.at[k], rc.at[k], m_send.at[k], c_recv.at[k], edge_dev)

    def d1_copy(c):
        k = c % SLOTS
        return remote(m_buf.at[k], rd1.at[k], m_send.at[k], d1_recv.at[k], mid_dev)

    def d2_copy(c):
        k = c % SLOTS
        return remote(rc.at[k], rd2.at[k], d2_send.at[k], d2_recv.at[k], mid_dev)

    def e_copy(c):
        k = c % 2
        return remote(e_buf.at[k], full.at[:, at(c)], e_send.at[k], e_recv.at[c], edge_dev)

    def l_copy(c):
        k = c % 2
        return remote(l_buf.at[k], lead.at[:, at(c)], l_send.at[k], l_recv.at[c], edge_dev)

    def k_copy(c):
        return pltpu.make_async_copy(k_buf.at[c % 2], full.at[:, at(c)], k_sem.at[c % 2])

    def lk_copy(c):
        return pltpu.make_async_copy(l_buf.at[c % 2], lead.at[:, at(c)], lk_sem.at[c % 2])

    def f_copy(c, d, from_hbm):
        src = lead.at[:, at(c)] if from_hbm else l_buf.at[c % 2]
        return remote(src, lead.at[:, at(c)], f_send.at[c % 2, d - 1], f_recv.at[c], (quarter * R + d, pcol))

    def g_copy(d):
        return remote(full.at[:, pl.ds(0, panel)], leading, g_send.at[d - 1], g_recv.at[0], (prow, d))

    def mix(mine, got, out, c, which):
        u = col_coef[which : which + 1, at(c)]
        v = col_coef[which + 1 : which + 2, at(c)]

        @pl.loop(0, rows // STRIP)
        def _(j):
            r = pl.ds(pl.multiple_of(j * STRIP, STRIP), STRIP)
            x = mine[r, :].astype(jnp.float32)
            y = got[r, :].astype(jnp.float32)
            out[r, :] = (u * x + v * y).astype(jnp.bfloat16)

    def combine(k, outs, strips):
        @pl.loop(0, strips)
        def _(j):
            r = pl.ds(pl.multiple_of(j * STRIP, STRIP), STRIP)
            w = row_coef[r, :]
            o = m_buf[k, r, :].astype(jnp.float32)
            n = rc[k, r, :].astype(jnp.float32)
            a = rd1[k, r, :].astype(jnp.float32)
            f = rd2[k, r, :].astype(jnp.float32)
            for out, b in outs:
                total = w[:, b : b + 1] * o + w[:, b + 1 : b + 2] * n
                total += w[:, b + 2 : b + 3] * a + w[:, b + 3 : b + 4] * f
                out[r, :] = total.astype(jnp.bfloat16)

    for c in range(3):
        load(c).start()
    for c in range(2):
        load(c).wait()
        a_copy(c).start()

    def body(i, carry):
        @pl.when(i + 3 < K)
        def _():
            load(i + 3).start()

        @pl.when(i + 2 < K)
        def _():
            c = i + 2
            load(c).wait()

            @pl.when(c >= SLOTS)
            def _():
                pl.semaphore_wait(cred_a, 1)

            a_copy(c).start()

        @pl.when(i < K)
        def _():
            c = i
            a_copy(c).wait_recv()

            @pl.when(c >= 2)
            def _():
                b_copy(c - 2).wait_send()

            mix(s_buf.at[c % SLOTS], ra.at[c % SLOTS], tb.at[c % 2], c, 0)
            a_copy(c).wait_send()

            @pl.when(c + SLOTS < K)
            def _():
                signal(cred_a, y_dev)

            @pl.when(c >= 2)
            def _():
                pl.semaphore_wait(cred_b, 1)

            b_copy(c).start()
            b_copy(c).wait_recv()

            @pl.when(outer & (c >= SLOTS))
            def _():
                c_copy(c - SLOTS).wait_send()

            mix(tb.at[c % 2], rb.at[c % 2], m_buf.at[c % SLOTS], c, 2)

            @pl.when(c + 2 < K)
            def _():
                signal(cred_b, core_dev)

            @pl.when(outer)
            def _():
                @pl.when(c >= SLOTS)
                def _():
                    pl.semaphore_wait(cred_c, 1)

                c_copy(c).start()

            @pl.when(inner)
            def _():
                @pl.when(c >= SLOTS)
                def _():
                    pl.semaphore_wait(cred_d, 1)

                d1_copy(c).start()

        @pl.when(inner & (i >= 1) & (i - 1 < K))
        def _():
            c = i - 1
            c_copy(c).wait_recv()
            d2_copy(c).start()

        @pl.when(inner & (i >= 3) & (i - 3 < K))
        def _():
            c = i - 3
            d1_copy(c).wait()
            d2_copy(c).wait()

            @pl.when(c >= 2)
            def _():
                e_copy(c - 2).wait_send()
                k_copy(c - 2).wait()

            combine(c % SLOTS, ((e_buf.at[c % 2], 0), (k_buf.at[c % 2], 4)), rows // STRIP)
            e_copy(c).start()
            k_copy(c).start()

            @pl.when(first_rank)
            def _():
                @pl.when(c >= 2)
                def _():
                    l_copy(c - 2).wait_send()
                    lk_copy(c - 2).wait()
                    for d in range(1, R):
                        f_copy(c - 2, d, False).wait_send()

                combine(c % SLOTS, ((l_buf.at[c % 2], 8),), panel // STRIP)
                l_copy(c).start()
                lk_copy(c).start()
                for d in range(1, R):
                    f_copy(c, d, False).start()

            @pl.when(c + SLOTS < K)
            def _():
                signal(cred_c, edge_dev)
                signal(cred_d, mid_dev)

        @pl.when(outer & (i >= LAST) & (i - LAST < K))
        def _():
            c = i - LAST
            e_copy(c).wait_recv()

            @pl.when(first_rank)
            def _():
                l_copy(c).wait_recv()

                @pl.when(c >= 2)
                def _():
                    for d in range(1, R):
                        f_copy(c - 2, d, True).wait_send()

                for d in range(1, R):
                    f_copy(c, d, True).start()

        @pl.when((pcol == 0) & (i == panel // width + 4))
        def _():
            for d in range(1, Q):
                g_copy(d).start()

        return carry

    lax.fori_loop(0, K + LAST, body, 0)

    for c in (K - 2, K - 1):
        b_copy(c).wait_send()

        @pl.when(inner)
        def _():
            e_copy(c).wait_send()
            k_copy(c).wait()

            @pl.when(first_rank)
            def _():
                l_copy(c).wait_send()
                lk_copy(c).wait()
                for d in range(1, R):
                    f_copy(c, d, False).wait_send()

        @pl.when(outer & first_rank)
        def _():
            for d in range(1, R):
                f_copy(c, d, True).wait_send()

    @pl.when(outer)
    def _():
        for c in range(K - SLOTS, K):
            c_copy(c).wait_send()

    @pl.when(rank > 0)
    def _():
        @pl.loop(0, K)
        def _(c):
            f_copy(c, 0, True).wait_recv() if R == 1 else f_copy(c, 1, True).wait_recv()

    @pl.when(pcol == 0)
    def _():
        for d in range(1, Q):
            g_copy(d).wait_send()

    @pl.when(pcol > 0)
    def _():
        g_copy(1).wait_recv()


def per_device(system, row_outer, row_inner, col_outer, col_inner, diag_inverse):
    panel = diag_inverse.shape[0]
    rows, cols = system.shape
    R = lax.axis_size("prow") // 4
    Q = lax.axis_size("pcol")
    C = Q // 4
    width = min(WIDTH, panel, cols // 8)
    K = cols // width
    f32, bf16 = jnp.float32, jnp.bfloat16
    assert lax.axis_size("prow") % 4 == 0 and Q % 4 == 0
    assert cols % width == 0 and panel % width == 0 and K >= panel // width + 4
    assert panel <= rows and panel % STRIP == 0 and rows % STRIP == 0
    quarter = lax.axis_index("prow") // R
    col_quarter = lax.axis_index("pcol") // C

    def hops(pairs):
        return [(a * R + r, b * R + r) for a, b in pairs for r in range(R)]

    is1 = quarter == 1
    own = jnp.stack([row_outer, row_inner])
    near = lax.ppermute(own, "prow", hops([(0, 1), (3, 2)]))
    other = lax.ppermute(jnp.concatenate([own, near]), "prow", hops([(1, 2), (2, 1)]))
    across, far = other[:2], other[2:]
    w0 = jnp.where(is1, near, far)
    w1 = jnp.where(is1, own, across)
    w2 = jnp.where(is1, across, own)
    w3 = jnp.where(is1, far, near)
    outer_a, inner_u = jnp.where(is1, w0, w2)
    outer_b, inner_d = jnp.where(is1, w1, w3)
    u0, u1 = 0.5 * inner_u * outer_a, 0.5 * inner_u * outer_b
    d0, d1 = 0.5 * inner_d * outer_a, 0.5 * inner_d * outer_b
    l0, l1 = 0.5 * w0[1] * w0[0], 0.5 * w0[1] * w1[0]
    one = jnp.stack([u1, u0, u0, u1, -d1, d0, d0, -d1, l1, l0, l0, l1])
    two = jnp.stack([-d0, d1, -d1, d0, -u0, -u1, u1, u0, l0, l1, l1, l0])
    row_coef = jnp.where(is1, one, two).T

    outer_c, inner_c = col_outer * root_half, col_inner * root_half
    col_coef = jnp.stack(
        [
            jnp.where(col_quarter < 2, outer_c, -outer_c),
            outer_c,
            jnp.where(col_quarter % 2 == 0, inner_c, -inner_c),
            inner_c,
        ]
    )

    dma = lambda *shape: pltpu.SemaphoreType.DMA(shape)
    block = lambda n, height: pltpu.VMEM((n, height, width), bf16)
    any_spec = pl.BlockSpec(memory_space=pl.ANY)
    vmem_spec = pl.BlockSpec(memory_space=pltpu.VMEM)
    full, lead, leading = pl.pallas_call(
        functools.partial(kernel, K, width, panel, R, Q),
        out_shape=(
            jax.ShapeDtypeStruct((rows, cols), bf16),
            jax.ShapeDtypeStruct((panel, cols), bf16),
            jax.ShapeDtypeStruct((rows, panel), bf16),
        ),
        in_specs=[any_spec, vmem_spec, vmem_spec],
        out_specs=(any_spec, any_spec, any_spec),
        scratch_shapes=[
            block(SLOTS, rows), block(SLOTS, rows), block(2, rows), block(2, rows),
            block(SLOTS, rows), block(SLOTS, rows), block(SLOTS, rows), block(SLOTS, rows),
            block(2, rows), block(2, rows), block(2, panel),
            dma(SLOTS), dma(SLOTS), dma(SLOTS), dma(2), dma(2), dma(SLOTS), dma(SLOTS), dma(SLOTS),
            dma(SLOTS), dma(SLOTS),
            dma(2), dma(K), dma(2), dma(K), dma(2), dma(2), dma(2, max(R - 1, 1)), dma(K), dma(Q - 1), dma(1),
            pltpu.SemaphoreType.REGULAR, pltpu.SemaphoreType.REGULAR,
            pltpu.SemaphoreType.REGULAR, pltpu.SemaphoreType.REGULAR,
        ],
        compiler_params=pltpu.CompilerParams(
            collective_id=0, has_side_effects=True, vmem_limit_bytes=60 * 1024 * 1024
        ),
    )(system, row_coef, col_coef)
    leading = jnp.where(lax.axis_index("pcol") == 0, full[:, :panel], leading)
    left = jnp.dot(leading, diag_inverse, preferred_element_type=f32).astype(bf16)
    update = jnp.dot(left, lead, preferred_element_type=f32)
    return (full.astype(f32) - update).astype(bf16)


def solution(mesh):
    in_specs = (P("prow", "pcol"), P("prow"), P("prow"), P("pcol"), P("pcol"), P())
    out_specs = P("prow", "pcol")
    return jax.shard_map(
        per_device, mesh=mesh, in_specs=in_specs, out_specs=out_specs, check_vma=False
    )
```

```python
import functools

import jax
import jax.numpy as jnp
from jax import lax
from jax.experimental import pallas as pl
from jax.experimental.pallas import tpu as pltpu
from jax.sharding import PartitionSpec as P

root_half = 0.7071067811865476
MESH = pl.DeviceIdType.MESH
WIDTH = 128
STRIP = 32
SLOTS = 4
LAST = 5


def kernel(
    K, width, panel, R, Q,
    system, own_w, col_coef,
    full, lead, leading,
    s_buf, ra, tb, rb, m_buf, rc, rd1, rd2, e_buf, k_buf, l_buf,
    load_sem, a_send, a_recv, b_send, b_recv, m_send, c_recv, d1_recv, d2_send, d2_recv,
    e_send, e_recv, l_send, l_recv, k_sem, lk_sem, f_send, f_recv, g_send, g_recv,
    cred_a, cred_b, cred_c, cred_d,
    near_w, across_w, far_w, w_tile, row_coef, w_send, w_recv,
):
    rows = system.shape[0]
    C = Q // 4
    prow = lax.axis_index("prow")
    pcol = lax.axis_index("pcol")
    quarter = prow // R
    rank = prow % R
    col_quarter = pcol // C
    inner = (quarter == 1) | (quarter == 2)
    outer = (quarter == 0) | (quarter == 3)
    first_rank = rank == 0

    y_dev = (prow, lax.rem(pcol + 2 * C, Q))
    core_dev = (prow, jnp.where(col_quarter % 2 == 0, pcol + C, pcol - C))
    edge_dev = (jnp.where(quarter % 2 == 0, prow + R, prow - R), pcol)
    mid_dev = ((3 - quarter) * R + rank, pcol)
    cross_dev = (lax.rem(quarter + 2, 4) * R + rank, pcol)

    def signal(sem, device):
        pl.semaphore_signal(sem, inc=1, device_id=device, device_id_type=MESH)

    barrier = pltpu.get_barrier_semaphore()
    for d in range(1, Q):
        signal(barrier, (prow, lax.rem(pcol + d, Q)))
    for d in range(1, R):
        signal(barrier, (quarter * R + lax.rem(rank + d, R), pcol))
    signal(barrier, edge_dev)
    signal(barrier, mid_dev)
    signal(barrier, cross_dev)
    pl.semaphore_wait(barrier, Q - 1 + R - 1 + 3)

    def at(c):
        return pl.ds(pl.multiple_of(c * width, width), width)

    def remote(src, dst, send, recv, device):
        return pltpu.make_async_remote_copy(
            src_ref=src, dst_ref=dst, send_sem=send, recv_sem=recv, device_id=device, device_id_type=MESH
        )

    def load(c):
        return pltpu.make_async_copy(system.at[:, at(c)], s_buf.at[c % SLOTS], load_sem.at[c % SLOTS])

    def a_copy(c):
        k = c % SLOTS
        return remote(s_buf.at[k], ra.at[k], a_send.at[k], a_recv.at[k], y_dev)

    def b_copy(c):
        k = c % 2
        return remote(tb.at[k], rb.at[k], b_send.at[k], b_recv.at[k], core_dev)

    def c_copy(c):
        k = c % SLOTS
        return remote(m_buf.at[k], rc.at[k], m_send.at[k], c_recv.at[k], edge_dev)

    def d1_copy(c):
        k = c % SLOTS
        return remote(m_buf.at[k], rd1.at[k], m_send.at[k], d1_recv.at[k], mid_dev)

    def d2_copy(c):
        k = c % SLOTS
        return remote(rc.at[k], rd2.at[k], d2_send.at[k], d2_recv.at[k], mid_dev)

    def e_copy(c):
        k = c % 2
        return remote(e_buf.at[k], full.at[:, at(c)], e_send.at[k], e_recv.at[c], edge_dev)

    def l_copy(c):
        k = c % 2
        return remote(l_buf.at[k], lead.at[:, at(c)], l_send.at[k], l_recv.at[c], edge_dev)

    def k_copy(c):
        return pltpu.make_async_copy(k_buf.at[c % 2], full.at[:, at(c)], k_sem.at[c % 2])

    def lk_copy(c):
        return pltpu.make_async_copy(l_buf.at[c % 2], lead.at[:, at(c)], lk_sem.at[c % 2])

    def f_copy(c, d, from_hbm):
        src = lead.at[:, at(c)] if from_hbm else l_buf.at[c % 2]
        return remote(src, lead.at[:, at(c)], f_send.at[c % 2, d - 1], f_recv.at[c], (quarter * R + d, pcol))

    def g_copy(d):
        return remote(full.at[:, pl.ds(0, panel)], leading, g_send.at[d - 1], g_recv.at[0], (prow, d))

    def mix(mine, got, out, c, which):
        u = col_coef[which : which + 1, at(c)]
        v = col_coef[which + 1 : which + 2, at(c)]

        @pl.loop(0, rows // STRIP)
        def _(j):
            r = pl.ds(pl.multiple_of(j * STRIP, STRIP), STRIP)
            x = mine[r, :].astype(jnp.float32)
            y = got[r, :].astype(jnp.float32)
            out[r, :] = (u * x + v * y).astype(jnp.bfloat16)

    def combine(k, outs, strips):
        @pl.loop(0, strips)
        def _(j):
            r = pl.ds(pl.multiple_of(j * STRIP, STRIP), STRIP)
            w = row_coef[r, :]
            o = m_buf[k, r, :].astype(jnp.float32)
            n = rc[k, r, :].astype(jnp.float32)
            a = rd1[k, r, :].astype(jnp.float32)
            f = rd2[k, r, :].astype(jnp.float32)
            for out, b in outs:
                total = w[:, b : b + 1] * o + w[:, b + 1 : b + 2] * n
                total += w[:, b + 2 : b + 3] * a + w[:, b + 3 : b + 4] * f
                out[r, :] = total.astype(jnp.bfloat16)

    for c in range(3):
        load(c).start()
    for c in range(2):
        load(c).wait()
        a_copy(c).start()

    near_copy = remote(own_w, near_w, w_send.at[0], w_recv.at[0], edge_dev)
    far_copy = remote(own_w, far_w, w_send.at[1], w_recv.at[1], cross_dev)
    across_copy = remote(own_w, across_w, w_send.at[2], w_recv.at[2], mid_dev)

    @pl.when(outer)
    def _():
        near_copy.start()
        far_copy.start()
        near_copy.wait_send()
        far_copy.wait_send()

    @pl.when(inner)
    def _():
        across_copy.start()
        across_copy.wait()
        near_copy.wait_recv()
        far_copy.wait_recv()
        is1 = quarter == 1
        w_tile[...] = jnp.zeros_like(w_tile)
        for j in range(rows // 128):
            b = slice(j * 128, (j + 1) * 128)
            level = []
            for n in range(2):
                o, e = own_w[n : n + 1, b], near_w[n : n + 1, b]
                a, f = across_w[n : n + 1, b], far_w[n : n + 1, b]
                level.append((jnp.where(is1, e, f), jnp.where(is1, o, a), jnp.where(is1, a, o), jnp.where(is1, f, e)))
            wo, wi = level
            outer_a, outer_b = jnp.where(is1, wo[0], wo[2]), jnp.where(is1, wo[1], wo[3])
            inner_u, inner_d = 0.5 * jnp.where(is1, wi[0], wi[2]), 0.5 * jnp.where(is1, wi[1], wi[3])
            u0, u1 = inner_u * outer_a, inner_u * outer_b
            d0, d1 = inner_d * outer_a, inner_d * outer_b
            l0, l1 = 0.5 * wi[0] * wo[0], 0.5 * wi[0] * wo[1]
            one = (u1, u0, u0, u1, -d1, d0, d0, -d1, l1, l0, l0, l1)
            two = (-d0, d1, -d1, d0, -u0, -u1, u1, u0, l0, l1, l1, l0)
            for n in range(12):
                w_tile[n : n + 1, :] = jnp.where(is1, one[n], two[n])
            row_coef[b, :] = w_tile[...].T

    def body(i, carry):
        @pl.when(i + 3 < K)
        def _():
            load(i + 3).start()

        @pl.when(i + 2 < K)
        def _():
            c = i + 2
            load(c).wait()

            @pl.when(c >= SLOTS)
            def _():
                pl.semaphore_wait(cred_a, 1)

            a_copy(c).start()

        @pl.when(i < K)
        def _():
            c = i
            a_copy(c).wait_recv()

            @pl.when(c >= 2)
            def _():
                b_copy(c - 2).wait_send()

            mix(s_buf.at[c % SLOTS], ra.at[c % SLOTS], tb.at[c % 2], c, 0)
            a_copy(c).wait_send()

            @pl.when(c + SLOTS < K)
            def _():
                signal(cred_a, y_dev)

            @pl.when(c >= 2)
            def _():
                pl.semaphore_wait(cred_b, 1)

            b_copy(c).start()
            b_copy(c).wait_recv()

            @pl.when(outer & (c >= SLOTS))
            def _():
                c_copy(c - SLOTS).wait_send()

            mix(tb.at[c % 2], rb.at[c % 2], m_buf.at[c % SLOTS], c, 2)

            @pl.when(c + 2 < K)
            def _():
                signal(cred_b, core_dev)

            @pl.when(outer)
            def _():
                @pl.when(c >= SLOTS)
                def _():
                    pl.semaphore_wait(cred_c, 1)

                c_copy(c).start()

            @pl.when(inner)
            def _():
                @pl.when(c >= SLOTS)
                def _():
                    pl.semaphore_wait(cred_d, 1)

                d1_copy(c).start()

        @pl.when(inner & (i >= 1) & (i - 1 < K))
        def _():
            c = i - 1
            c_copy(c).wait_recv()
            d2_copy(c).start()

        @pl.when(inner & (i >= 3) & (i - 3 < K))
        def _():
            c = i - 3
            d1_copy(c).wait()
            d2_copy(c).wait()

            @pl.when(c >= 2)
            def _():
                e_copy(c - 2).wait_send()
                k_copy(c - 2).wait()

            combine(c % SLOTS, ((e_buf.at[c % 2], 0), (k_buf.at[c % 2], 4)), rows // STRIP)
            e_copy(c).start()
            k_copy(c).start()

            @pl.when(first_rank)
            def _():
                @pl.when(c >= 2)
                def _():
                    l_copy(c - 2).wait_send()
                    lk_copy(c - 2).wait()
                    for d in range(1, R):
                        f_copy(c - 2, d, False).wait_send()

                combine(c % SLOTS, ((l_buf.at[c % 2], 8),), panel // STRIP)
                l_copy(c).start()
                lk_copy(c).start()
                for d in range(1, R):
                    f_copy(c, d, False).start()

            @pl.when(c + SLOTS < K)
            def _():
                signal(cred_c, edge_dev)
                signal(cred_d, mid_dev)

        @pl.when(outer & (i >= LAST) & (i - LAST < K))
        def _():
            c = i - LAST
            e_copy(c).wait_recv()

            @pl.when(first_rank)
            def _():
                l_copy(c).wait_recv()

                @pl.when(c >= 2)
                def _():
                    for d in range(1, R):
                        f_copy(c - 2, d, True).wait_send()

                for d in range(1, R):
                    f_copy(c, d, True).start()

        @pl.when((pcol == 0) & (i == panel // width + 4))
        def _():
            for d in range(1, Q):
                g_copy(d).start()

        return carry

    lax.fori_loop(0, K + LAST, body, 0)

    for c in (K - 2, K - 1):
        b_copy(c).wait_send()

        @pl.when(inner)
        def _():
            e_copy(c).wait_send()
            k_copy(c).wait()

            @pl.when(first_rank)
            def _():
                l_copy(c).wait_send()
                lk_copy(c).wait()
                for d in range(1, R):
                    f_copy(c, d, False).wait_send()

        @pl.when(outer & first_rank)
        def _():
            for d in range(1, R):
                f_copy(c, d, True).wait_send()

    @pl.when(outer)
    def _():
        for c in range(K - SLOTS, K):
            c_copy(c).wait_send()

    @pl.when(rank > 0)
    def _():
        @pl.loop(0, K)
        def _(c):
            f_copy(c, 0, True).wait_recv() if R == 1 else f_copy(c, 1, True).wait_recv()

    @pl.when(pcol == 0)
    def _():
        for d in range(1, Q):
            g_copy(d).wait_send()

    @pl.when(pcol > 0)
    def _():
        g_copy(1).wait_recv()


def per_device(system, row_outer, row_inner, col_outer, col_inner, diag_inverse):
    panel = diag_inverse.shape[0]
    rows, cols = system.shape
    R = lax.axis_size("prow") // 4
    Q = lax.axis_size("pcol")
    C = Q // 4
    width = min(WIDTH, panel, cols // 8)
    K = cols // width
    f32, bf16 = jnp.float32, jnp.bfloat16
    assert lax.axis_size("prow") % 4 == 0 and Q % 4 == 0
    assert cols % width == 0 and panel % width == 0 and K >= panel // width + 4
    assert panel <= rows and panel % STRIP == 0 and rows % STRIP == 0 and rows % 128 == 0
    col_quarter = lax.axis_index("pcol") // C
    own_w = jnp.concatenate([row_outer[None], row_inner[None], jnp.zeros((6, rows), f32)])
    outer_c, inner_c = col_outer * root_half, col_inner * root_half
    col_coef = jnp.stack(
        [
            jnp.where(col_quarter < 2, outer_c, -outer_c),
            outer_c,
            jnp.where(col_quarter % 2 == 0, inner_c, -inner_c),
            inner_c,
        ]
    )

    dma = lambda *shape: pltpu.SemaphoreType.DMA(shape)
    block = lambda n, height: pltpu.VMEM((n, height, width), bf16)
    any_spec = pl.BlockSpec(memory_space=pl.ANY)
    vmem_spec = pl.BlockSpec(memory_space=pltpu.VMEM)
    full, lead, leading = pl.pallas_call(
        functools.partial(kernel, K, width, panel, R, Q),
        out_shape=(
            jax.ShapeDtypeStruct((rows, cols), bf16),
            jax.ShapeDtypeStruct((panel, cols), bf16),
            jax.ShapeDtypeStruct((rows, panel), bf16),
        ),
        in_specs=[any_spec, vmem_spec, vmem_spec],
        out_specs=(any_spec, any_spec, any_spec),
        scratch_shapes=[
            block(SLOTS, rows), block(SLOTS, rows), block(2, rows), block(2, rows),
            block(SLOTS, rows), block(SLOTS, rows), block(SLOTS, rows), block(SLOTS, rows),
            block(2, rows), block(2, rows), block(2, panel),
            dma(SLOTS), dma(SLOTS), dma(SLOTS), dma(2), dma(2), dma(SLOTS), dma(SLOTS), dma(SLOTS),
            dma(SLOTS), dma(SLOTS),
            dma(2), dma(K), dma(2), dma(K), dma(2), dma(2), dma(2, max(R - 1, 1)), dma(K), dma(Q - 1), dma(1),
            pltpu.SemaphoreType.REGULAR, pltpu.SemaphoreType.REGULAR,
            pltpu.SemaphoreType.REGULAR, pltpu.SemaphoreType.REGULAR,
            pltpu.VMEM((8, rows), f32), pltpu.VMEM((8, rows), f32), pltpu.VMEM((8, rows), f32),
            pltpu.VMEM((128, 128), f32), pltpu.VMEM((rows, 128), f32), dma(3), dma(3),
        ],
        compiler_params=pltpu.CompilerParams(
            collective_id=0, has_side_effects=True, vmem_limit_bytes=60 * 1024 * 1024
        ),
    )(system, own_w, col_coef)
    leading = jnp.where(lax.axis_index("pcol") == 0, full[:, :panel], leading)
    left = jnp.dot(leading, diag_inverse, preferred_element_type=f32).astype(bf16)
    update = jnp.dot(left, lead, preferred_element_type=f32)
    return (full.astype(f32) - update).astype(bf16)


def solution(mesh):
    in_specs = (P("prow", "pcol"), P("prow"), P("prow"), P("pcol"), P("pcol"), P())
    out_specs = P("prow", "pcol")
    return jax.shard_map(
        per_device, mesh=mesh, in_specs=in_specs, out_specs=out_specs, check_vma=False
    )
```
